512 devices in a mesh: rows: 128 (over y, z, core), cols: 4 (over x).
Axes of the slice: x: 4, y: 8, z: 8, core: 2. Of those that a mesh axis runs over, the one named last changes fastest.
Arguments:
- tile_values: float32 [1920, 256, 256], P('rows'), may hold values from -0.09375 to 0.09375, as said below
- tile_rows: int32 [1920], P('rows'), may hold values from 0 to 1
- tile_cols: int32 [1920], P('rows'), may hold values from -1 to 255, as said below
- start_vectors: float32 [128, 65536], P('cols', 'rows'), may hold values from -6 to 6
Outputs:
- vectors: float32 [128, 65536], P('cols', 'rows')
- images: float32 [128, 65536], P('cols', 'rows')
The draws below stay inside these ranges and needn't reach their ends.
Inputs may be any that keep to these rules, and one draw needn't show every extreme that they name: tile_values lie within the stated bounds. `tile_cols`: if slot s of index p of rows is not empty, its column block lies on index p + s // 3 - 2 of rows, that is in 2 * (p + s // 3 - 2) up to 2 * (p + s // 3 - 1) - 1; slots whose index would fall off the mesh are empty.
All inputs are finite; a program needn't handle non-finite values.
Results may differ from the reference program's by a relative error of at most 0.0001.
Values sent between devices are 32-bit elements; how exact they have to be, the bound alone decides.
No kernel may reach another device: no remote copies, remote signals or barrier semaphores. Data moves between devices by JAX's collectives and lax.ppermute only.
A program may use at most 64 MiB of HBM per device.

```python
import jax
import jax.numpy as jnp
from jax import lax

TILE = 256
K = 128
RB = 2
REACH = 2
GROUP = 3
ITERS = 3
SLOTS = 15
NBLK = 256
BOXES = 65536
NTILES = 1920
N_ROWS = 128


def draw_tile_values(key, part):
    slot_index = jnp.arange(NTILES)
    device = (slot_index // SLOTS).astype(jnp.float32)
    scales = 1.0 + 2.0 * device / max(N_ROWS - 1, 1)
    amplitude = 8.0 / TILE
    base = jax.random.uniform(key, (NTILES, TILE, TILE), jnp.float32, -1.0, 1.0)
    return amplitude * scales[:, None, None] * base


def draw_tile_cols(key, part):
    key_count = jax.random.fold_in(key, 11)
    key_slot = jax.random.fold_in(key, 12)
    key_block = jax.random.fold_in(key, 13)
    slot_index = jnp.arange(NTILES, dtype=jnp.int32)
    device = slot_index // SLOTS
    slot_pos = slot_index % SLOTS
    target = device + slot_pos // GROUP - REACH
    live_count = jax.random.randint(key_count, (N_ROWS,), SLOTS // 2, SLOTS + 1)[device]
    slot_draw = jax.random.randint(key_slot, (NTILES,), 0, SLOTS)
    block_pick = jax.random.randint(key_block, (NTILES,), 0, RB)
    is_live = (slot_draw < live_count) & (target >= 0) & (target < N_ROWS)
    return jnp.where(is_live, target * RB + block_pick, -1).astype(jnp.int32)


def place_ends(entries, rng, low, largest):
    shape = entries.shape
    spot = [jax.random.randint(jax.random.fold_in(rng, axis), (), 0, shape[axis]) for axis in range(len(shape))]
    entries = entries.at[tuple(spot)].set(low)
    longest = shape.index(max(shape))
    spot[longest] = (spot[longest] + 1) % shape[longest]
    return entries.at[tuple(spot)].set(largest)


def steps_of(own_key, shape, cuts, smallest, largest):
    def one(dim, blocks):
        steps = jax.random.uniform(jax.random.fold_in(jax.random.fold_in(own_key, 6), dim), (blocks,), jnp.float32, smallest / len(cuts), largest / len(cuts))
        return jnp.repeat(jnp.exp(steps), shape[dim] // blocks).reshape((-1,) + (1,) * (len(shape) - dim - 1))

    level = one(*cuts[0])
    for cut in cuts[1:]:
        level = level * one(*cut)
    return level


def normal_values(key, shape, spread, limit, cuts=(), held_as=jnp.bfloat16):
    entries = jax.random.normal(key, shape, jnp.float32) * spread
    if len(cuts) > 0:
        entries = steps_of(key, shape, cuts, -0.22, 0.18) * entries
    return jnp.clip(entries, min=-limit, max=limit).astype(held_as)


def setup_inputs(seed: int = 0) -> dict:
    key_list = jax.random.split(jax.random.key(seed), 5)
    tile_values = draw_tile_values(jax.random.fold_in(key_list[4], 71), 0)
    tile_rows = place_ends(jax.random.randint(key_list[1], (NTILES,), 0, RB), jax.random.fold_in(key_list[1], 1), 0, RB - 1).astype(jnp.int32)
    tile_cols = draw_tile_cols(jax.random.fold_in(key_list[4], 71), 0)
    start_vectors = normal_values(key_list[3], (K, BOXES), 1.0, 6.0, ((0, 4), (1, 128)), jnp.float32)
    return {"tile_values": tile_values, "tile_rows": tile_rows, "tile_cols": tile_cols, "start_vectors": start_vectors}


highest = lax.Precision.HIGHEST

def reference(tile_values, tile_rows, tile_cols, start_vectors):
    slot_index = jnp.arange(NTILES, dtype=jnp.int32)
    device = slot_index // SLOTS
    is_live = tile_cols >= 0
    row_global = (device * RB + tile_rows).astype(jnp.int32)
    col_global = jnp.where(is_live, tile_cols, 0).astype(jnp.int32)
    weights = is_live.astype(jnp.float32)
    stacked = (tile_values.reshape(N_ROWS, SLOTS, TILE, TILE), row_global.reshape(N_ROWS, SLOTS), col_global.reshape(N_ROWS, SLOTS), weights.reshape(N_ROWS, SLOTS))

    def forward(vectors):
        blocks_in = vectors.reshape(K, NBLK, TILE).transpose(1, 0, 2)

        def visit(totals, item):
            values, rows, cols, mask = item
            chosen = blocks_in[cols]
            product = jnp.einsum('skt,sat->ska', chosen, values, precision=highest) * mask[:, None, None]
            return (totals.at[rows].add(product), None)
        totals, unused = lax.scan(visit, jnp.zeros((NBLK, K, TILE), jnp.float32), stacked)
        return totals.transpose(1, 0, 2).reshape(K, BOXES)

    def adjoint(images):
        blocks_in = images.reshape(K, NBLK, TILE).transpose(1, 0, 2)

        def visit(totals, item):
            values, rows, cols, mask = item
            chosen = blocks_in[rows]
            product = jnp.einsum('ska,sat->skt', chosen, values, precision=highest) * mask[:, None, None]
            return (totals.at[cols].add(product), None)
        totals, unused = lax.scan(visit, jnp.zeros((NBLK, K, TILE), jnp.float32), stacked)
        return totals.transpose(1, 0, 2).reshape(K, BOXES)
    vectors = start_vectors
    images = start_vectors
    for iteration in range(ITERS):
        images = forward(vectors)
        pulled = adjoint(images)
        gram_full = jnp.dot(pulled, pulled.T, precision=highest)
        factor = jnp.linalg.cholesky(gram_full)
        inverse = jax.scipy.linalg.solve_triangular(factor, jnp.eye(K, dtype=jnp.float32), lower=True)
        vectors = jnp.sqrt(jnp.float32(BOXES)) * jnp.dot(inverse, pulled, precision=highest)
    return (vectors, images)
```

```python
import jax
import jax.numpy as jnp
from jax import lax
from jax.sharding import Mesh, PartitionSpec as P

REACH = 2
ITERS = 3
ROWS = ("y", "z", "core")

precise = lax.Precision.HIGHEST


def shifted(value, steps):
    count = lax.axis_size(ROWS)
    leading, last = (max(0, -steps), min(count, count - steps))
    return lax.ppermute(value, ROWS, [(source, source + steps) for source in range(leading, last)])


def operator_rows(tile_values, tile_rows, tile_cols, blocks):
    slots, tile_size, _ = tile_values.shape
    groups = 2 * REACH + 1
    in_group = slots // groups
    is_live = tile_cols >= 0
    col_local = jnp.where(is_live, tile_cols % blocks, -1)
    bands = []
    for r in range(blocks):
        pieces = []
        for group_idx in range(groups):
            for c in range(blocks):
                total = 0.0
                for s in range(group_idx * in_group, (group_idx + 1) * in_group):
                    hit = (tile_rows[s] == r) & (col_local[s] == c)
                    total = total + jnp.where(hit, tile_values[s], 0.0)
                pieces.append(total)
        bands.append(jnp.concatenate(pieces, axis=1))
    return jnp.concatenate(bands, axis=0)


def spread(value, axes):
    count = lax.axis_size(axes)
    copies = jnp.broadcast_to(value[None], (count, *value.shape))
    return lax.all_to_all(copies, axes, 0, 0)


def body(tile_values, tile_rows, tile_cols, start_vectors):
    tile_size = tile_values.shape[1]
    local_cols, row_width = start_vectors.shape
    blocks = row_width // tile_size
    groups = 2 * REACH + 1
    x_count = lax.axis_size("x")
    all_count = local_cols * x_count
    boxes_total = row_width * lax.axis_size(ROWS)
    col_start = lax.axis_index("x") * local_cols
    band = operator_rows(tile_values, tile_rows, tile_cols, blocks)
    vectors = start_vectors
    images = start_vectors
    for iteration in range(ITERS):
        nearby = [
            vectors if g == REACH else shifted(vectors, REACH - g) for g in range(groups)
        ]
        nearby = jnp.concatenate(nearby, axis=1)
        images = lax.dot_general(nearby, band, (((1,), (1,)), ((), ())), precision=precise)
        sent = jnp.dot(images, band, precision=precise)
        pulled = sent[:, REACH * row_width : (REACH + 1) * row_width]
        for g in range(groups):
            if g != REACH:
                pulled = pulled + shifted(sent[:, g * row_width : (g + 1) * row_width], g - REACH)
        all_cols = spread(pulled, "x").reshape(all_count, row_width)
        gram = jnp.dot(pulled, all_cols.T, precision=precise)
        gram = jnp.sum(spread(gram, ("z", "core")), axis=0)
        gram = spread(gram, ("y", "x"))
        gram = gram.reshape(-1, x_count, local_cols, all_count).sum(axis=0).reshape(all_count, all_count)
        factor = jnp.linalg.cholesky(gram)
        inverse = jax.scipy.linalg.solve_triangular(
            factor, jnp.eye(all_count, dtype=jnp.float32), lower=True
        )
        own_rows = lax.dynamic_slice_in_dim(inverse, col_start, local_cols, 0)
        vectors = jnp.sqrt(jnp.float32(boxes_total)) * jnp.dot(own_rows, all_cols, precision=precise)
    return (vectors, images)


def solution(mesh):
    split = Mesh(mesh.devices.reshape(8, 8, 2, 4), ("y", "z", "core", "x"))
    return jax.shard_map(
        body,
        mesh=split,
        in_specs=(P(ROWS, None, None), P(ROWS), P(ROWS), P("x", ROWS)),
        out_specs=(P("x", ROWS), P("x", ROWS)),
        check_vma=False,
    )
```

```python
import functools

import jax
import jax.numpy as jnp
from jax import lax
from jax.experimental import pallas as pl
from jax.experimental.pallas import tpu as pltpu
from jax.sharding import Mesh, PartitionSpec as P

REACH = 2
GROUPS = 2 * REACH + 1
ITERS = 3
ROWS = ("y", "z", "core")
MIB = 1 << 20

precise = lax.Precision.HIGHEST


def halves(value):
    high = value.astype(jnp.bfloat16)
    low = (value - high.astype(jnp.float32)).astype(jnp.bfloat16)
    return high, low


def band_kernel(rows_ref, cols_ref, tiles_ref, high_ref, low_ref, total):
    group = pl.program_id(0)
    in_group, size, _ = tiles_ref.shape
    blocks = total.shape[0] // size
    total[...] = jnp.zeros_like(total)
    for s in range(in_group):
        row, col = rows_ref[group * in_group + s], cols_ref[group * in_group + s]

        @pl.when(col >= 0)
        def _():
            at = (
                pl.ds(pl.multiple_of(row * size, size), size),
                pl.ds(pl.multiple_of(lax.rem(col, blocks) * size, size), size),
            )
            total[at] += tiles_ref[s]

    high_ref[0], low_ref[0] = halves(total[...])


def operator_band(tile_values, tile_rows, tile_cols, width):
    slots, size, _ = tile_values.shape
    in_group = slots // GROUPS
    piece = jax.ShapeDtypeStruct((GROUPS, width, width), jnp.bfloat16)
    return pl.pallas_call(
        band_kernel,
        grid_spec=pltpu.PrefetchScalarGridSpec(
            num_scalar_prefetch=2,
            grid=(GROUPS,),
            in_specs=[pl.BlockSpec((in_group, size, size), lambda g, rows, cols: (g, 0, 0))],
            out_specs=[pl.BlockSpec((1, width, width), lambda g, rows, cols: (g, 0, 0))] * 2,
            scratch_shapes=[pltpu.VMEM((width, width), jnp.float32)],
        ),
        out_shape=[piece, piece],
        compiler_params=pltpu.CompilerParams(vmem_limit_bytes=20 * MIB),
        name="operator_band",
    )(tile_rows, tile_cols, tile_values)


def products(high, low, band_high, band_low, dims):
    count = high.shape[0]
    dot = functools.partial(
        lax.dot_general, dimension_numbers=(dims, ((), ())), preferred_element_type=jnp.float32
    )
    both = dot(jnp.concatenate([high, low], axis=0), band_high)
    return both[:count] + both[count:] + dot(high, band_low)


def apply_kernel(core_ref, below, above, own, got, high_hbm, low_hbm, images, kept, crossing, down, up, high, low, sems):
    core = core_ref[0]
    copies = []
    for g in range(GROUPS):
        pair = [
            pltpu.make_async_copy(high_hbm.at[g], high.at[g], sems.at[0, g]),
            pltpu.make_async_copy(low_hbm.at[g], low.at[g], sems.at[1, g]),
        ]
        for copy in pair:
            copy.start()
        copies.append(pair)
    near = [below[...], got[1 - core], own[...], got[core], above[...]]
    total = 0.0
    for g in range(GROUPS):
        for copy in copies[g]:
            copy.wait()
        total = total + products(*halves(near[g]), high[g], low[g], ((1,), (1,)))
    images[...] = total
    parts = halves(total)
    sent = [products(*parts, high[g], low[g], ((1,), (0,))) for g in range(GROUPS)]
    down[...] = sent[0]
    crossing[1 - core] = sent[1]
    kept[...] = sent[2]
    crossing[core] = sent[3]
    up[...] = sent[4]


def apply_operator(core, below, above, own, got, high, low):
    vmem, hbm = pl.BlockSpec(memory_space=pltpu.VMEM), pl.BlockSpec(memory_space=pl.ANY)
    one = jax.ShapeDtypeStruct(own.shape, jnp.float32)
    two = jax.ShapeDtypeStruct(got.shape, jnp.float32)
    return pl.pallas_call(
        apply_kernel,
        in_specs=[pl.BlockSpec(memory_space=pltpu.SMEM)] + [vmem] * 4 + [hbm] * 2,
        out_specs=[vmem] * 5,
        out_shape=[one, one, two, one, one],
        scratch_shapes=[
            pltpu.VMEM(high.shape, high.dtype),
            pltpu.VMEM(low.shape, low.dtype),
            pltpu.SemaphoreType.DMA((2, GROUPS)),
        ],
        compiler_params=pltpu.CompilerParams(vmem_limit_bytes=16 * MIB),
        name="apply_operator",
    )(core, below, above, own, got, high, low)


def gram_kernel(place_ref, all_ref, out_ref, whole):
    total = lax.dot_general(
        all_ref[...],
        all_ref[...],
        (((1,), (1,)), ((), ())),
        precision=precise,
        preferred_element_type=jnp.float32,
    )
    whole[...] = total.reshape(whole.shape)
    few = out_ref.shape[1]
    for k in range(whole.shape[1] // few):

        @pl.when(place_ref[0] == k)
        def _():
            out_ref[...] = whole[:, few * k : few * (k + 1), :]


def gram_share(place, all_vectors, runs, x_count):
    vmem = pl.BlockSpec(memory_space=pltpu.VMEM)
    size = all_vectors.shape[0]
    run = size // runs
    return pl.pallas_call(
        gram_kernel,
        in_specs=[pl.BlockSpec(memory_space=pltpu.SMEM), vmem],
        out_specs=vmem,
        out_shape=jax.ShapeDtypeStruct((runs, run // x_count, size), jnp.float32),
        scratch_shapes=[pltpu.VMEM((runs, run, size), jnp.float32)],
        compiler_params=pltpu.CompilerParams(vmem_limit_bytes=8 * MIB),
        name="gram_share",
    )(place, all_vectors)


def whiten_kernel(place_ref, gram_ref, all_ref, out_ref, zero_ref, inverse_ref, *, scale, panel):
    size = gram_ref.shape[0]
    tall = 8
    zero_ref[...] = jnp.zeros((tall, size), jnp.float32)
    zero = zero_ref[...]
    row = lax.broadcasted_iota(jnp.int32, (tall, size), 0)
    col = lax.broadcasted_iota(jnp.int32, (tall, size), 1)
    count = size // tall
    left = [gram_ref[tall * b : tall * (b + 1), :] for b in range(count)]
    right = [jnp.where(row + tall * b == col, 1.0, 0.0).astype(jnp.float32) for b in range(count)]

    def lane(value, j):
        return jnp.broadcast_to(value[:, j : j + 1], (tall, size))

    def line(value, i):
        return jnp.broadcast_to(value[i : i + 1, :], (tall, size))

    pivots = jnp.ones((tall, size), jnp.float32)
    for j in range(0, size, panel):
        jb, js = divmod(j, tall)
        low = jb if js + panel < tall else jb + 1
        a = [line(left[jb], js + k) for k in range(panel)]
        w = [line(right[jb], js + k) for k in range(panel)]
        c = [[lane(left[b], j + k) for b in range(low, count)] for k in range(panel)]
        s = {(k, i): lane(a[k] + zero, j + i) for k in range(panel) for i in range(k, panel)}
        factors = []
        for k in range(panel):
            inv = 1.0 / s[k, k]
            pivots = jnp.where(row == js + k, s[k, k], pivots)
            for i in range(k + 1, panel):
                f = s[k, i] * inv
                for i2 in range(i, panel):
                    s[i, i2] = s[i, i2] - f * s[k, i2]
                a[i] = a[i] - f * a[k]
                w[i] = w[i] - f * w[k]
            m = [value * inv for value in c[k]]
            factors.append(m)
            for k2 in range(k + 1, panel):
                c[k2] = [y - x * s[k, k2] for x, y in zip(m, c[k2])]
        for n, b in enumerate(range(low, count)):
            da = dw = 0.0
            for k in range(panel):
                m = factors[k][n]
                if b == jb:
                    m = jnp.where(row > js + panel - 1, m, 0.0)
                da = da + m * a[k]
                dw = dw + m * w[k]
            left[b] = left[b] - da
            right[b] = right[b] - dw
        for k in range(1, panel):
            left[jb] = jnp.where(row == js + k, a[k], left[jb])
            right[jb] = jnp.where(row == js + k, w[k], right[jb])
        if js + panel == tall:
            inverse_ref[tall * jb : tall * (jb + 1), :] = right[jb] * (1.0 / jnp.sqrt(pivots))
            pivots = jnp.ones((tall, size), jnp.float32)
    own = out_ref.shape[0]
    rows = inverse_ref[pl.ds(pl.multiple_of(place_ref[0] * own, own), own), :]
    out_ref[...] = scale * jnp.dot(rows, all_ref[...], precision=precise, preferred_element_type=jnp.float32)


def whiten(place, gram, all_vectors, own, scale):
    vmem = pl.BlockSpec(memory_space=pltpu.VMEM)
    size = gram.shape[0]
    return pl.pallas_call(
        functools.partial(whiten_kernel, scale=scale, panel=4),
        in_specs=[pl.BlockSpec(memory_space=pltpu.SMEM), vmem, vmem],
        out_specs=vmem,
        out_shape=jax.ShapeDtypeStruct((own, all_vectors.shape[1]), jnp.float32),
        scratch_shapes=[pltpu.VMEM((8, size), jnp.float32), pltpu.VMEM((size, size), jnp.float32)],
        compiler_params=pltpu.CompilerParams(vmem_limit_bytes=8 * MIB),
        name="whiten",
    )(place, gram, all_vectors)


def shifted(value, steps):
    count = lax.axis_size(ROWS)
    leading, last = (max(0, -steps), min(count, count - steps))
    return lax.ppermute(value, ROWS, [(source, source + steps) for source in range(leading, last)])


def swapped(value):
    return lax.ppermute(value, "core", [(0, 1), (1, 0)])


def spread(value, axes):
    count = lax.axis_size(axes)
    copies = jnp.broadcast_to(value[None], (count, *value.shape))
    return lax.all_to_all(copies, axes, 0, 0)


def summed_gram(place, all_vectors):
    line, x_count = lax.axis_size(("z", "core")), lax.axis_size("x")
    size = all_vectors.shape[0]
    share = gram_share(place, all_vectors, line, x_count)
    few = share.shape[1]
    share = lax.all_to_all(share, ("z", "core"), 0, 0).sum(axis=0)
    run = spread(share, ("y", "x")).reshape(-1, x_count * few, size).sum(axis=0)
    return spread(run, ("z", "core")).reshape(size, size)


def body(tile_values, tile_rows, tile_cols, start_vectors):
    local_cols, row_width = start_vectors.shape
    all_count = local_cols * lax.axis_size("x")
    scale = (row_width * lax.axis_size(ROWS)) ** 0.5
    core = lax.axis_index("core").astype(jnp.int32)
    first = core == 0
    place = lax.axis_index("x").astype(jnp.int32).reshape(1)
    core = core.reshape(1)
    high, low = operator_band(tile_values, tile_rows, tile_cols, row_width)
    vectors = start_vectors
    for iteration in range(ITERS):
        below, above = shifted(vectors, 2), shifted(vectors, -2)
        got = swapped(jnp.stack([vectors, jnp.where(first, above, below)]))
        images, kept, crossing, down, up = apply_operator(core, below, above, vectors, got, high, low)
        got = swapped(crossing)
        up = jnp.where(first, up + got[1], up)
        down = jnp.where(first, down, down + got[1])
        pulled = kept + got[0] + shifted(up, 2) + shifted(down, -2)
        all_vectors = spread(pulled, "x").reshape(all_count, row_width)
        gram = summed_gram(place, all_vectors)
        vectors = whiten(place, gram, all_vectors, local_cols, scale)
    return (vectors, images)


def solution(mesh):
    split = Mesh(mesh.devices.reshape(8, 8, 2, 4), ("y", "z", "core", "x"))
    return jax.shard_map(
        body,
        mesh=split,
        in_specs=(P(ROWS, None, None), P(ROWS), P(ROWS), P("x", ROWS)),
        out_specs=(P("x", ROWS), P("x", ROWS)),
        check_vma=False,
    )
```

```python
import functools

import jax
import jax.numpy as jnp
from jax import lax
from jax.experimental import pallas as pl
from jax.experimental.pallas import tpu as pltpu
from jax.sharding import Mesh, PartitionSpec as P

REACH = 2
GROUPS = 2 * REACH + 1
ITERS = 3
ROWS = ("y", "z", "core")
MIB = 1 << 20

precise = lax.Precision.HIGHEST


def halves(value):
    high = value.astype(jnp.bfloat16)
    low = (value - high.astype(jnp.float32)).astype(jnp.bfloat16)
    return high, low


def band_kernel(rows_ref, cols_ref, tiles_ref, high_ref, low_ref, total):
    group = pl.program_id(0)
    in_group, size, _ = tiles_ref.shape
    blocks = total.shape[0] // size
    total[...] = jnp.zeros_like(total)
    for s in range(in_group):
        row, col = rows_ref[group * in_group + s], cols_ref[group * in_group + s]

        @pl.when(col >= 0)
        def _():
            at = (
                pl.ds(pl.multiple_of(row * size, size), size),
                pl.ds(pl.multiple_of(lax.rem(col, blocks) * size, size), size),
            )
            total[at] += tiles_ref[s]

    high_ref[0], low_ref[0] = halves(total[...])


def operator_band(tile_values, tile_rows, tile_cols, width):
    slots, size, _ = tile_values.shape
    in_group = slots // GROUPS
    piece = jax.ShapeDtypeStruct((GROUPS, width, width), jnp.bfloat16)
    return pl.pallas_call(
        band_kernel,
        grid_spec=pltpu.PrefetchScalarGridSpec(
            num_scalar_prefetch=2,
            grid=(GROUPS,),
            in_specs=[pl.BlockSpec((in_group, size, size), lambda g, rows, cols: (g, 0, 0))],
            out_specs=[pl.BlockSpec((1, width, width), lambda g, rows, cols: (g, 0, 0))] * 2,
            scratch_shapes=[pltpu.VMEM((width, width), jnp.float32)],
        ),
        out_shape=[piece, piece],
        name="operator_band",
    )(tile_rows, tile_cols, tile_values)


def products(high, low, band_high, band_low, dims):
    count = high.shape[0]
    dot = functools.partial(
        lax.dot_general, dimension_numbers=(dims, ((), ())), preferred_element_type=jnp.float32
    )
    both = dot(jnp.concatenate([high, low], axis=0), band_high)
    return both[:count] + both[count:] + dot(high, band_low)


def apply_kernel(core_ref, below, above, own, got, high_hbm, low_hbm, images, kept, crossing, down, up, high, low, sems):
    core = core_ref[0]
    copies = []
    for g in range(GROUPS):
        pair = [
            pltpu.make_async_copy(high_hbm.at[g], high.at[g], sems.at[0, g]),
            pltpu.make_async_copy(low_hbm.at[g], low.at[g], sems.at[1, g]),
        ]
        for copy in pair:
            copy.start()
        copies.append(pair)
    near = [below[...], got[1 - core], own[...], got[core], above[...]]
    total = 0.0
    for g in range(GROUPS):
        for copy in copies[g]:
            copy.wait()
        total = total + products(*halves(near[g]), high[g], low[g], ((1,), (1,)))
    images[...] = total
    parts = halves(total)
    sent = [products(*parts, high[g], low[g], ((1,), (0,))) for g in range(GROUPS)]
    down[...] = sent[0]
    crossing[1 - core] = sent[1]
    kept[...] = sent[2]
    crossing[core] = sent[3]
    up[...] = sent[4]


def apply_operator(core, below, above, own, got, high, low):
    vmem, hbm = pl.BlockSpec(memory_space=pltpu.VMEM), pl.BlockSpec(memory_space=pltpu.HBM)
    one = jax.ShapeDtypeStruct(own.shape, jnp.float32)
    two = jax.ShapeDtypeStruct(got.shape, jnp.float32)
    return pl.pallas_call(
        apply_kernel,
        in_specs=[pl.BlockSpec(memory_space=pltpu.SMEM)] + [vmem] * 4 + [hbm] * 2,
        out_specs=[vmem] * 5,
        out_shape=[one, one, two, one, one],
        scratch_shapes=[
            pltpu.VMEM(high.shape, high.dtype),
            pltpu.VMEM(low.shape, low.dtype),
            pltpu.SemaphoreType.DMA((2, GROUPS)),
        ],
        compiler_params=pltpu.CompilerParams(vmem_limit_bytes=16 * MIB),
        name="apply_operator",
    )(core, below, above, own, got, high, low)


def gram_of(value):
    return lax.dot_general(
        value, value, (((1,), (1,)), ((), ())), precision=precise, preferred_element_type=jnp.float32
    )


def gram_kernel(all_ref, out_ref):
    out_ref[...] = gram_of(all_ref[...])


def gram_share(all_vectors):
    vmem = pl.BlockSpec(memory_space=pltpu.VMEM)
    size = all_vectors.shape[0]
    return pl.pallas_call(
        gram_kernel,
        in_specs=[vmem],
        out_specs=vmem,
        out_shape=jax.ShapeDtypeStruct((size, size), jnp.float32),
        compiler_params=pltpu.CompilerParams(vmem_limit_bytes=8 * MIB),
        name="gram_share",
    )(all_vectors)


def advance_kernel(place_ref, inverse_ref, raw_ref, all_ref, own_ref, gram_ref, *, scale):
    members, parts, own, width = raw_ref.shape
    dot = functools.partial(jnp.dot, precision=precise, preferred_element_type=jnp.float32)
    current = scale * dot(inverse_ref[...], raw_ref[:, 0].reshape(members * own, width))
    all_ref[...] = current
    gram_ref[...] = gram_of(current)
    rows = pl.ds(pl.multiple_of(place_ref[0] * own, own), own)
    if parts == 1:
        own_ref[...] = all_ref[rows, :]
    else:
        last = raw_ref[:, parts - 1].reshape(members * own, width)
        own_ref[...] = scale * dot(inverse_ref[rows, :], last)


def advance(place, inverse, raw, scale):
    vmem = pl.BlockSpec(memory_space=pltpu.VMEM)
    members, _, own, width = raw.shape
    size = members * own
    return pl.pallas_call(
        functools.partial(advance_kernel, scale=scale),
        in_specs=[pl.BlockSpec(memory_space=pltpu.SMEM), vmem, vmem],
        out_specs=[vmem] * 3,
        out_shape=[
            jax.ShapeDtypeStruct((size, width), jnp.float32),
            jax.ShapeDtypeStruct((own, width), jnp.float32),
            jax.ShapeDtypeStruct((size, size), jnp.float32),
        ],
        compiler_params=pltpu.CompilerParams(vmem_limit_bytes=8 * MIB),
        name="advance",
    )(place, inverse, raw)


def invert(gram_ref, inverse_ref, zero_ref, panel):
    size = gram_ref.shape[0]
    tall = 8
    zero_ref[...] = jnp.zeros((tall, size), jnp.float32)
    zero = zero_ref[...]
    row = lax.broadcasted_iota(jnp.int32, (tall, size), 0)
    col = lax.broadcasted_iota(jnp.int32, (tall, size), 1)
    count = size // tall
    left = [gram_ref[tall * b : tall * (b + 1), :] for b in range(count)]
    right = [jnp.where(row + tall * b == col, 1.0, 0.0).astype(jnp.float32) for b in range(count)]

    def lane(value, j):
        return jnp.broadcast_to(value[:, j : j + 1], (tall, size))

    def line(value, i):
        return jnp.broadcast_to(value[i : i + 1, :], (tall, size))

    pivots = jnp.ones((tall, size), jnp.float32)
    for j in range(0, size, panel):
        jb, js = divmod(j, tall)
        low = jb if js + panel < tall else jb + 1
        a = [line(left[jb], js + k) for k in range(panel)]
        w = [line(right[jb], js + k) for k in range(panel)]
        c = [[lane(left[b], j + k) for b in range(low, count)] for k in range(panel)]
        s = {(k, i): lane(a[k] + zero, j + i) for k in range(panel) for i in range(k, panel)}
        factors = []
        for k in range(panel):
            inv = 1.0 / s[k, k]
            pivots = jnp.where(row == js + k, s[k, k], pivots)
            for i in range(k + 1, panel):
                f = s[k, i] * inv
                for i2 in range(i, panel):
                    s[i, i2] = s[i, i2] - f * s[k, i2]
                a[i] = a[i] - f * a[k]
                w[i] = w[i] - f * w[k]
            m = [value * inv for value in c[k]]
            factors.append(m)
            for k2 in range(k + 1, panel):
                c[k2] = [y - x * s[k, k2] for x, y in zip(m, c[k2])]
        for n, b in enumerate(range(low, count)):
            da = dw = 0.0
            for k in range(panel):
                m = factors[k][n]
                if b == jb:
                    m = jnp.where(row > js + panel - 1, m, 0.0)
                da = da + m * a[k]
                dw = dw + m * w[k]
            left[b] = left[b] - da
            right[b] = right[b] - dw
        for k in range(1, panel):
            left[jb] = jnp.where(row == js + k, a[k], left[jb])
            right[jb] = jnp.where(row == js + k, w[k], right[jb])
        if js + panel == tall:
            inverse_ref[tall * jb : tall * (jb + 1), :] = right[jb] * (1.0 / jnp.sqrt(pivots))
            pivots = jnp.ones((tall, size), jnp.float32)


def inverse_kernel(gram_ref, inverse_ref, zero_ref, *, panel):
    invert(gram_ref, inverse_ref, zero_ref, panel)


def cholesky_inverse(gram):
    vmem = pl.BlockSpec(memory_space=pltpu.VMEM)
    return pl.pallas_call(
        functools.partial(inverse_kernel, panel=4),
        in_specs=[vmem],
        out_specs=vmem,
        out_shape=jax.ShapeDtypeStruct(gram.shape, jnp.float32),
        scratch_shapes=[pltpu.VMEM((8, gram.shape[0]), jnp.float32)],
        compiler_params=pltpu.CompilerParams(vmem_limit_bytes=8 * MIB),
        name="cholesky_inverse",
    )(gram)


def whiten_kernel(place_ref, gram_ref, all_ref, out_ref, zero_ref, inverse_ref, *, scale, panel):
    invert(gram_ref, inverse_ref, zero_ref, panel)
    own = out_ref.shape[0]
    rows = inverse_ref[pl.ds(pl.multiple_of(place_ref[0] * own, own), own), :]
    out_ref[...] = scale * jnp.dot(rows, all_ref[...], precision=precise, preferred_element_type=jnp.float32)


def whiten(place, gram, all_vectors, own, scale):
    vmem = pl.BlockSpec(memory_space=pltpu.VMEM)
    size = gram.shape[0]
    return pl.pallas_call(
        functools.partial(whiten_kernel, scale=scale, panel=4),
        in_specs=[pl.BlockSpec(memory_space=pltpu.SMEM), vmem, vmem],
        out_specs=vmem,
        out_shape=jax.ShapeDtypeStruct((own, all_vectors.shape[1]), jnp.float32),
        scratch_shapes=[pltpu.VMEM((8, size), jnp.float32), pltpu.VMEM((size, size), jnp.float32)],
        compiler_params=pltpu.CompilerParams(vmem_limit_bytes=8 * MIB),
        name="whiten",
    )(place, gram, all_vectors)


def shifted(value, steps):
    count = lax.axis_size(ROWS)
    leading, last = (max(0, -steps), min(count, count - steps))
    return lax.ppermute(value, ROWS, [(source, source + steps) for source in range(leading, last)])


def swapped(value):
    return lax.ppermute(value, "core", [(0, 1), (1, 0)])


def spread(value, axes):
    count = lax.axis_size(axes)
    copies = jnp.broadcast_to(value[None], (count, *value.shape))
    return lax.all_to_all(copies, axes, 0, 0)


def summed(share):
    size = share.shape[0]
    line = lax.axis_size(("z", "core"))
    share = lax.all_to_all(share.reshape(line, size // line, size), ("z", "core"), 0, 0).sum(axis=0)
    run = spread(share, "y").sum(axis=0)
    return spread(run, ("z", "core")).reshape(size, size)


def body(tile_values, tile_rows, tile_cols, start_vectors):
    own, row_width = start_vectors.shape
    all_count = own * lax.axis_size("x")
    scale = (row_width * lax.axis_size(ROWS)) ** 0.5
    core = lax.axis_index("core").astype(jnp.int32)
    first = core == 0
    place = lax.axis_index("x").astype(jnp.int32).reshape(1)
    core = core.reshape(1)
    high, low = operator_band(tile_values, tile_rows, tile_cols, row_width)

    def operator_pass(vectors):
        below, above = shifted(vectors, 2), shifted(vectors, -2)
        got = swapped(jnp.stack([vectors, jnp.where(first, above, below)]))
        images, kept, crossing, down, up = apply_operator(core, below, above, vectors, got, high, low)
        got = swapped(crossing)
        up = jnp.where(first, up + got[1], up)
        down = jnp.where(first, down, down + got[1])
        return images, kept + got[0] + shifted(up, 2) + shifted(down, -2)

    images, pulled = operator_pass(start_vectors)
    all_vectors = spread(pulled, "x").reshape(all_count, row_width)
    gram = gram_share(all_vectors)
    for iteration in range(1, ITERS):
        images, ahead = operator_pass(pulled)
        inverse = cholesky_inverse(summed(gram))
        parts = [ahead, images] if iteration == ITERS - 1 else [ahead]
        raw = spread(jnp.stack(parts), "x")
        all_vectors, pulled, gram = advance(place, inverse, raw, scale)
    images = pulled
    vectors = whiten(place, summed(gram), all_vectors, own, scale)
    return (vectors, images)


def solution(mesh):
    split = Mesh(mesh.devices.reshape(8, 8, 2, 4), ("y", "z", "core", "x"))
    return jax.shard_map(
        body,
        mesh=split,
        in_specs=(P(ROWS, None, None), P(ROWS), P(ROWS), P("x", ROWS)),
        out_specs=(P("x", ROWS), P("x", ROWS)),
        check_vma=False,
    )
```

```python
import functools

import jax
import jax.numpy as jnp
from jax import lax
from jax.experimental import pallas as pl
from jax.experimental.pallas import tpu as pltpu
from jax.sharding import Mesh, PartitionSpec as P

REACH = 2
GROUPS = 2 * REACH + 1
ITERS = 3
ROWS = ("y", "z", "core")
MIB = 1 << 20

precise = lax.Precision.HIGHEST


def halves(value):
    high = value.astype(jnp.bfloat16)
    low = (value - high.astype(jnp.float32)).astype(jnp.bfloat16)
    return high, low


def band_kernel(rows_ref, cols_ref, tiles_hbm, high_hbm, low_hbm, tiles, total, high, low, sems):
    groups, width, _ = high.shape
    slots, size, _ = tiles.shape
    in_group, blocks = slots // groups, width // size
    arrive = []
    for g in range(groups):
        part = pl.ds(g * in_group, in_group)
        arrive.append(pltpu.make_async_copy(tiles_hbm.at[part], tiles.at[part], sems.at[0, g]))
        arrive[-1].start()
    leave = []
    for g in range(groups):
        arrive[g].wait()
        total[...] = jnp.zeros_like(total)
        for s in range(in_group):
            slot = g * in_group + s
            row, col = rows_ref[slot], cols_ref[slot]

            @pl.when(col >= 0)
            def _():
                at = (
                    pl.ds(pl.multiple_of(row * size, size), size),
                    pl.ds(pl.multiple_of(lax.rem(col, blocks) * size, size), size),
                )
                total[at] += tiles[slot]

        high[g], low[g] = halves(total[...])
        leave += [
            pltpu.make_async_copy(high.at[g], high_hbm.at[g], sems.at[1, g]),
            pltpu.make_async_copy(low.at[g], low_hbm.at[g], sems.at[2, g]),
        ]
        leave[-2].start()
        leave[-1].start()
    for copy in leave:
        copy.wait()


def operator_band(tile_values, tile_rows, tile_cols, width):
    smem, hbm = pl.BlockSpec(memory_space=pltpu.SMEM), pl.BlockSpec(memory_space=pl.ANY)
    piece = jax.ShapeDtypeStruct((GROUPS, width, width), jnp.bfloat16)
    return pl.pallas_call(
        band_kernel,
        in_specs=[smem, smem, hbm],
        out_specs=[hbm, hbm],
        out_shape=[piece, piece],
        scratch_shapes=[
            pltpu.VMEM(tile_values.shape, jnp.float32),
            pltpu.VMEM((width, width), jnp.float32),
            pltpu.VMEM(piece.shape, piece.dtype),
            pltpu.VMEM(piece.shape, piece.dtype),
            pltpu.SemaphoreType.DMA((3, GROUPS)),
        ],
        compiler_params=pltpu.CompilerParams(vmem_limit_bytes=63 * MIB),
        name="operator_band",
    )(tile_rows, tile_cols, tile_values)


def products(high, low, band_high, band_low, dims):
    count = high.shape[0]
    dot = functools.partial(
        lax.dot_general, dimension_numbers=(dims, ((), ())), preferred_element_type=jnp.float32
    )
    both = dot(jnp.concatenate([high, low], axis=0), band_high)
    return both[:count] + both[count:] + dot(high, band_low)


def apply_kernel(core_ref, below, above, own, got, high_hbm, low_hbm, images, kept, crossing, down, up, high, low, sems):
    core = core_ref[0]
    copies = []
    for g in range(GROUPS):
        pair = [
            pltpu.make_async_copy(high_hbm.at[g], high.at[g], sems.at[0, g]),
            pltpu.make_async_copy(low_hbm.at[g], low.at[g], sems.at[1, g]),
        ]
        for copy in pair:
            copy.start()
        copies.append(pair)
    near = [below[...], got[1 - core], own[...], got[core], above[...]]
    total = 0.0
    for g in range(GROUPS):
        for copy in copies[g]:
            copy.wait()
        total = total + products(*halves(near[g]), high[g], low[g], ((1,), (1,)))
    images[...] = total
    parts = halves(total)
    sent = [products(*parts, high[g], low[g], ((1,), (0,))) for g in range(GROUPS)]
    down[...] = sent[0]
    crossing[1 - core] = sent[1]
    kept[...] = sent[2]
    crossing[core] = sent[3]
    up[...] = sent[4]


def apply_operator(core, below, above, own, got, high, low):
    vmem, hbm = pl.BlockSpec(memory_space=pltpu.VMEM), pl.BlockSpec(memory_space=pl.ANY)
    one = jax.ShapeDtypeStruct(own.shape, jnp.float32)
    two = jax.ShapeDtypeStruct(got.shape, jnp.float32)
    return pl.pallas_call(
        apply_kernel,
        in_specs=[pl.BlockSpec(memory_space=pltpu.SMEM)] + [vmem] * 4 + [hbm] * 2,
        out_specs=[vmem] * 5,
        out_shape=[one, one, two, one, one],
        scratch_shapes=[
            pltpu.VMEM(high.shape, high.dtype),
            pltpu.VMEM(low.shape, low.dtype),
            pltpu.SemaphoreType.DMA((2, GROUPS)),
        ],
        compiler_params=pltpu.CompilerParams(vmem_limit_bytes=32 * MIB),
        name="apply_operator",
    )(core, below, above, own, got, high, low)


def gram_of(value):
    return lax.dot_general(
        value, value, (((1,), (1,)), ((), ())), precision=precise, preferred_element_type=jnp.float32
    )


def gram_kernel(all_ref, out_ref):
    out_ref[...] = gram_of(all_ref[...])


def gram_share(all_vectors):
    vmem = pl.BlockSpec(memory_space=pltpu.VMEM)
    size = all_vectors.shape[0]
    return pl.pallas_call(
        gram_kernel,
        in_specs=[vmem],
        out_specs=vmem,
        out_shape=jax.ShapeDtypeStruct((size, size), jnp.float32),
        compiler_params=pltpu.CompilerParams(vmem_limit_bytes=8 * MIB),
        name="gram_share",
    )(all_vectors)


def advance_kernel(place_ref, inverse_ref, raw_ref, all_ref, own_ref, gram_ref, *, scale):
    members, parts, own, width = raw_ref.shape
    dot = functools.partial(jnp.dot, precision=precise, preferred_element_type=jnp.float32)
    current = scale * dot(inverse_ref[...], raw_ref[:, 0].reshape(members * own, width))
    all_ref[...] = current
    gram_ref[...] = gram_of(current)
    rows = pl.ds(pl.multiple_of(place_ref[0] * own, own), own)
    if parts == 1:
        own_ref[...] = all_ref[rows, :]
    else:
        last = raw_ref[:, parts - 1].reshape(members * own, width)
        own_ref[...] = scale * dot(inverse_ref[rows, :], last)


def advance(place, inverse, raw, scale):
    vmem = pl.BlockSpec(memory_space=pltpu.VMEM)
    members, _, own, width = raw.shape
    size = members * own
    return pl.pallas_call(
        functools.partial(advance_kernel, scale=scale),
        in_specs=[pl.BlockSpec(memory_space=pltpu.SMEM), vmem, vmem],
        out_specs=[vmem] * 3,
        out_shape=[
            jax.ShapeDtypeStruct((size, width), jnp.float32),
            jax.ShapeDtypeStruct((own, width), jnp.float32),
            jax.ShapeDtypeStruct((size, size), jnp.float32),
        ],
        compiler_params=pltpu.CompilerParams(vmem_limit_bytes=8 * MIB),
        name="advance",
    )(place, inverse, raw)


def invert(gram_ref, inverse_ref, zero_ref, panel):
    size = gram_ref.shape[0]
    tall = 8
    zero_ref[...] = jnp.zeros((tall, size), jnp.float32)
    zero = zero_ref[...]
    row = lax.broadcasted_iota(jnp.int32, (tall, size), 0)
    col = lax.broadcasted_iota(jnp.int32, (tall, size), 1)
    count = size // tall
    left = [gram_ref[tall * b : tall * (b + 1), :] for b in range(count)]
    right = [jnp.where(row + tall * b == col, 1.0, 0.0).astype(jnp.float32) for b in range(count)]

    def lane(value, j):
        return jnp.broadcast_to(value[:, j : j + 1], (tall, size))

    def line(value, i):
        return jnp.broadcast_to(value[i : i + 1, :], (tall, size))

    pivots = jnp.ones((tall, size), jnp.float32)
    for j in range(0, size, panel):
        jb, js = divmod(j, tall)
        low = jb if js + panel < tall else jb + 1
        a = [line(left[jb], js + k) for k in range(panel)]
        w = [line(right[jb], js + k) for k in range(panel)]
        c = [[lane(left[b], j + k) for b in range(low, count)] for k in range(panel)]
        s = {(k, i): lane(a[k] + zero, j + i) for k in range(panel) for i in range(k, panel)}
        factors = []
        for k in range(panel):
            inv = 1.0 / s[k, k]
            pivots = jnp.where(row == js + k, s[k, k], pivots)
            for i in range(k + 1, panel):
                f = s[k, i] * inv
                for i2 in range(i, panel):
                    s[i, i2] = s[i, i2] - f * s[k, i2]
                a[i] = a[i] - f * a[k]
                w[i] = w[i] - f * w[k]
            m = [value * inv for value in c[k]]
            factors.append(m)
            for k2 in range(k + 1, panel):
                c[k2] = [y - x * s[k, k2] for x, y in zip(m, c[k2])]
        for n, b in enumerate(range(low, count)):
            da = dw = 0.0
            for k in range(panel):
                m = factors[k][n]
                if b == jb:
                    m = jnp.where(row > js + panel - 1, m, 0.0)
                da = da + m * a[k]
                dw = dw + m * w[k]
            left[b] = left[b] - da
            right[b] = right[b] - dw
        for k in range(1, panel):
            left[jb] = jnp.where(row == js + k, a[k], left[jb])
            right[jb] = jnp.where(row == js + k, w[k], right[jb])
        if js + panel == tall:
            inverse_ref[tall * jb : tall * (jb + 1), :] = right[jb] * (1.0 / jnp.sqrt(pivots))
            pivots = jnp.ones((tall, size), jnp.float32)


def inverse_kernel(gram_ref, inverse_ref, zero_ref, *, panel):
    invert(gram_ref, inverse_ref, zero_ref, panel)


def cholesky_inverse(gram):
    vmem = pl.BlockSpec(memory_space=pltpu.VMEM)
    return pl.pallas_call(
        functools.partial(inverse_kernel, panel=4),
        in_specs=[vmem],
        out_specs=vmem,
        out_shape=jax.ShapeDtypeStruct(gram.shape, jnp.float32),
        scratch_shapes=[pltpu.VMEM((8, gram.shape[0]), jnp.float32)],
        compiler_params=pltpu.CompilerParams(vmem_limit_bytes=8 * MIB),
        name="cholesky_inverse",
    )(gram)


def whiten_kernel(place_ref, gram_ref, all_ref, out_ref, zero_ref, inverse_ref, *, scale, panel):
    invert(gram_ref, inverse_ref, zero_ref, panel)
    own = out_ref.shape[0]
    rows = inverse_ref[pl.ds(pl.multiple_of(place_ref[0] * own, own), own), :]
    out_ref[...] = scale * jnp.dot(rows, all_ref[...], precision=precise, preferred_element_type=jnp.float32)


def whiten(place, gram, all_vectors, own, scale):
    vmem = pl.BlockSpec(memory_space=pltpu.VMEM)
    size = gram.shape[0]
    return pl.pallas_call(
        functools.partial(whiten_kernel, scale=scale, panel=4),
        in_specs=[pl.BlockSpec(memory_space=pltpu.SMEM), vmem, vmem],
        out_specs=vmem,
        out_shape=jax.ShapeDtypeStruct((own, all_vectors.shape[1]), jnp.float32),
        scratch_shapes=[pltpu.VMEM((8, size), jnp.float32), pltpu.VMEM((size, size), jnp.float32)],
        compiler_params=pltpu.CompilerParams(vmem_limit_bytes=8 * MIB),
        name="whiten",
    )(place, gram, all_vectors)


def shifted(value, steps):
    count = lax.axis_size(ROWS)
    leading, last = (max(0, -steps), min(count, count - steps))
    return lax.ppermute(value, ROWS, [(source, source + steps) for source in range(leading, last)])


def swapped(value):
    return lax.ppermute(value, "core", [(0, 1), (1, 0)])


def spread(value, axes):
    count = lax.axis_size(axes)
    copies = jnp.broadcast_to(value[None], (count, *value.shape))
    return lax.all_to_all(copies, axes, 0, 0)


def scattered(whole):
    size = whole.shape[0]
    line = lax.axis_size(("z", "core"))
    return lax.all_to_all(whole.reshape(line, size // line, size), ("z", "core"), 0, 0).sum(axis=0)


def gathered(share):
    size = share.shape[1]
    run = spread(share, "y").sum(axis=0)
    return spread(run, ("z", "core")).reshape(size, size)


def body(tile_values, tile_rows, tile_cols, start_vectors):
    own, row_width = start_vectors.shape
    all_count = own * lax.axis_size("x")
    scale = (row_width * lax.axis_size(ROWS)) ** 0.5
    core = lax.axis_index("core").astype(jnp.int32)
    first = core == 0
    place = lax.axis_index("x").astype(jnp.int32).reshape(1)
    core = core.reshape(1)
    bands = operator_band(tile_values, tile_rows, tile_cols, row_width)

    def operator_pass(vectors, beside=()):
        below, above = shifted(vectors, 2), shifted(vectors, -2)
        below, above, *beside = lax.optimization_barrier((below, above, *beside))
        got = swapped(jnp.stack([vectors, jnp.where(first, above, below)]))
        images, kept, crossing, down, up = apply_operator(core, below, above, vectors, got, *bands)
        got = swapped(crossing)
        up = jnp.where(first, up + got[1], up)
        down = jnp.where(first, down, down + got[1])
        return images, kept + got[0] + shifted(up, 2) + shifted(down, -2), beside

    images, pulled, bands = operator_pass(start_vectors, bands)
    all_vectors = spread(pulled, "x").reshape(all_count, row_width)
    share = scattered(gram_share(all_vectors))
    for iteration in range(1, ITERS):
        last = iteration == ITERS - 1
        images, ahead, taken = operator_pass(pulled, [share] if last else [])
        inverse = cholesky_inverse(gathered(*(taken or [share])))
        raw = spread(jnp.stack([ahead, images] if last else [ahead]), "x")
        all_vectors, pulled, gram = advance(place, inverse, raw, scale)
        share = scattered(gram)
    images = pulled
    vectors = whiten(place, gathered(share), all_vectors, own, scale)
    return (vectors, images)


def solution(mesh):
    split = Mesh(mesh.devices.reshape(8, 8, 2, 4), ("y", "z", "core", "x"))
    return jax.shard_map(
        body,
        mesh=split,
        in_specs=(P(ROWS, None, None), P(ROWS), P(ROWS), P("x", ROWS)),
        out_specs=(P("x", ROWS), P("x", ROWS)),
        check_vma=False,
    )
```

```python
import functools

import jax
import jax.numpy as jnp
from jax import lax
from jax.experimental import pallas as pl
from jax.experimental.pallas import tpu as pltpu
from jax.sharding import Mesh, PartitionSpec as P

REACH = 2
GROUPS = 2 * REACH + 1
ITERS = 3
ROWS = ("y", "z", "core")
MIB = 1 << 20

precise = lax.Precision.HIGHEST


def halves(value):
    high = value.astype(jnp.bfloat16)
    low = (value - high.astype(jnp.float32)).astype(jnp.bfloat16)
    return high, low


def band_kernel(rows_ref, cols_ref, tiles_hbm, high, low, tiles, total, sems):
    groups, width, _ = high.shape
    slots, size, _ = tiles.shape
    in_group, blocks = slots // groups, width // size
    arrive = []
    for g in range(groups):
        part = pl.ds(g * in_group, in_group)
        arrive.append(pltpu.make_async_copy(tiles_hbm.at[part], tiles.at[part], sems.at[g]))
        arrive[-1].start()
    for g in range(groups):
        arrive[g].wait()
        total[...] = jnp.zeros_like(total)
        for s in range(in_group):
            slot = g * in_group + s
            row, col = rows_ref[slot], cols_ref[slot]

            @pl.when(col >= 0)
            def _():
                at = (
                    pl.ds(pl.multiple_of(row * size, size), size),
                    pl.ds(pl.multiple_of(lax.rem(col, blocks) * size, size), size),
                )
                total[at] += tiles[slot]

        high[g], low[g] = halves(total[...])


def operator_band(tile_values, tile_rows, tile_cols, width):
    smem, vmem = pl.BlockSpec(memory_space=pltpu.SMEM), pl.BlockSpec(memory_space=pltpu.VMEM)
    piece = jax.ShapeDtypeStruct((GROUPS, width, width), jnp.bfloat16)
    return pl.pallas_call(
        band_kernel,
        in_specs=[smem, smem, pl.BlockSpec(memory_space=pl.ANY)],
        out_specs=[vmem, vmem],
        out_shape=[piece, piece],
        scratch_shapes=[
            pltpu.VMEM(tile_values.shape, jnp.float32),
            pltpu.VMEM((width, width), jnp.float32),
            pltpu.SemaphoreType.DMA((GROUPS,)),
        ],
        compiler_params=pltpu.CompilerParams(vmem_limit_bytes=48 * MIB),
        name="operator_band",
    )(tile_rows, tile_cols, tile_values)


def products(high, low, band_high, band_low, dims):
    count = high.shape[0]
    dot = functools.partial(
        lax.dot_general, dimension_numbers=(dims, ((), ())), preferred_element_type=jnp.float32
    )
    both = dot(jnp.concatenate([high, low], axis=0), band_high)
    return both[:count] + both[count:] + dot(high, band_low)


def apply_kernel(core_ref, below, above, own, got, high, low, images, kept, crossing, down, up):
    core = core_ref[0]
    near = [below[...], got[1 - core], own[...], got[core], above[...]]
    total = 0.0
    for g in range(GROUPS):
        total = total + products(*halves(near[g]), high[g], low[g], ((1,), (1,)))
    images[...] = total
    parts = halves(total)
    sent = [products(*parts, high[g], low[g], ((1,), (0,))) for g in range(GROUPS)]
    down[...] = sent[0]
    crossing[1 - core] = sent[1]
    kept[...] = sent[2]
    crossing[core] = sent[3]
    up[...] = sent[4]


def apply_operator(core, below, above, own, got, high, low):
    vmem = pl.BlockSpec(memory_space=pltpu.VMEM)
    one = jax.ShapeDtypeStruct(own.shape, jnp.float32)
    two = jax.ShapeDtypeStruct(got.shape, jnp.float32)
    return pl.pallas_call(
        apply_kernel,
        in_specs=[pl.BlockSpec(memory_space=pltpu.SMEM)] + [vmem] * 6,
        out_specs=[vmem] * 5,
        out_shape=[one, one, two, one, one],
        compiler_params=pltpu.CompilerParams(vmem_limit_bytes=16 * MIB),
        name="apply_operator",
    )(core, below, above, own, got, high, low)


def gram_of(value):
    return lax.dot_general(
        value, value, (((1,), (1,)), ((), ())), precision=precise, preferred_element_type=jnp.float32
    )


def gram_kernel(all_ref, out_ref):
    out_ref[...] = gram_of(all_ref[...])


def gram_share(all_vectors):
    vmem = pl.BlockSpec(memory_space=pltpu.VMEM)
    size = all_vectors.shape[0]
    return pl.pallas_call(
        gram_kernel,
        in_specs=[vmem],
        out_specs=vmem,
        out_shape=jax.ShapeDtypeStruct((size, size), jnp.float32),
        compiler_params=pltpu.CompilerParams(vmem_limit_bytes=8 * MIB),
        name="gram_share",
    )(all_vectors)


def advance_kernel(place_ref, inverse_ref, raw_ref, all_ref, own_ref, gram_ref, *, scale):
    members, parts, own, width = raw_ref.shape
    dot = functools.partial(jnp.dot, precision=precise, preferred_element_type=jnp.float32)
    current = scale * dot(inverse_ref[...], raw_ref[:, 0].reshape(members * own, width))
    all_ref[...] = current
    gram_ref[...] = gram_of(current)
    rows = pl.ds(pl.multiple_of(place_ref[0] * own, own), own)
    if parts == 1:
        own_ref[...] = all_ref[rows, :]
    else:
        last = raw_ref[:, parts - 1].reshape(members * own, width)
        own_ref[...] = scale * dot(inverse_ref[rows, :], last)


def advance(place, inverse, raw, scale):
    vmem = pl.BlockSpec(memory_space=pltpu.VMEM)
    members, _, own, width = raw.shape
    size = members * own
    return pl.pallas_call(
        functools.partial(advance_kernel, scale=scale),
        in_specs=[pl.BlockSpec(memory_space=pltpu.SMEM), vmem, vmem],
        out_specs=[vmem] * 3,
        out_shape=[
            jax.ShapeDtypeStruct((size, width), jnp.float32),
            jax.ShapeDtypeStruct((own, width), jnp.float32),
            jax.ShapeDtypeStruct((size, size), jnp.float32),
        ],
        compiler_params=pltpu.CompilerParams(vmem_limit_bytes=8 * MIB),
        name="advance",
    )(place, inverse, raw)


def invert(gram_ref, inverse_ref, zero_ref, panel):
    size = gram_ref.shape[0]
    tall = 8
    zero_ref[...] = jnp.zeros((tall, size), jnp.float32)
    zero = zero_ref[...]
    row = lax.broadcasted_iota(jnp.int32, (tall, size), 0)
    col = lax.broadcasted_iota(jnp.int32, (tall, size), 1)
    count = size // tall
    left = [gram_ref[tall * b : tall * (b + 1), :] for b in range(count)]
    right = [jnp.where(row + tall * b == col, 1.0, 0.0).astype(jnp.float32) for b in range(count)]

    def lane(value, j):
        return jnp.broadcast_to(value[:, j : j + 1], (tall, size))

    def line(value, i):
        return jnp.broadcast_to(value[i : i + 1, :], (tall, size))

    pivots = jnp.ones((tall, size), jnp.float32)
    for j in range(0, size, panel):
        jb, js = divmod(j, tall)
        low = jb if js + panel < tall else jb + 1
        a = [line(left[jb], js + k) for k in range(panel)]
        w = [line(right[jb], js + k) for k in range(panel)]
        c = [[lane(left[b], j + k) for b in range(low, count)] for k in range(panel)]
        s = {(k, i): lane(a[k] + zero, j + i) for k in range(panel) for i in range(k, panel)}
        factors = []
        for k in range(panel):
            inv = 1.0 / s[k, k]
            pivots = jnp.where(row == js + k, s[k, k], pivots)
            for i in range(k + 1, panel):
                f = s[k, i] * inv
                for i2 in range(i, panel):
                    s[i, i2] = s[i, i2] - f * s[k, i2]
                a[i] = a[i] - f * a[k]
                w[i] = w[i] - f * w[k]
            m = [value * inv for value in c[k]]
            factors.append(m)
            for k2 in range(k + 1, panel):
                c[k2] = [y - x * s[k, k2] for x, y in zip(m, c[k2])]
        for n, b in enumerate(range(low, count)):
            da = dw = 0.0
            for k in range(panel):
                m = factors[k][n]
                if b == jb:
                    m = jnp.where(row > js + panel - 1, m, 0.0)
                da = da + m * a[k]
                dw = dw + m * w[k]
            left[b] = left[b] - da
            right[b] = right[b] - dw
        for k in range(1, panel):
            left[jb] = jnp.where(row == js + k, a[k], left[jb])
            right[jb] = jnp.where(row == js + k, w[k], right[jb])
        if js + panel == tall:
            inverse_ref[tall * jb : tall * (jb + 1), :] = right[jb] * (1.0 / jnp.sqrt(pivots))
            pivots = jnp.ones((tall, size), jnp.float32)


def inverse_kernel(gram_ref, inverse_ref, zero_ref, *, panel):
    invert(gram_ref, inverse_ref, zero_ref, panel)


def cholesky_inverse(gram):
    vmem = pl.BlockSpec(memory_space=pltpu.VMEM)
    return pl.pallas_call(
        functools.partial(inverse_kernel, panel=4),
        in_specs=[vmem],
        out_specs=vmem,
        out_shape=jax.ShapeDtypeStruct(gram.shape, jnp.float32),
        scratch_shapes=[pltpu.VMEM((8, gram.shape[0]), jnp.float32)],
        compiler_params=pltpu.CompilerParams(vmem_limit_bytes=8 * MIB),
        name="cholesky_inverse",
    )(gram)


def whiten_kernel(place_ref, gram_ref, all_ref, out_ref, zero_ref, inverse_ref, *, scale, panel):
    invert(gram_ref, inverse_ref, zero_ref, panel)
    own = out_ref.shape[0]
    rows = inverse_ref[pl.ds(pl.multiple_of(place_ref[0] * own, own), own), :]
    out_ref[...] = scale * jnp.dot(rows, all_ref[...], precision=precise, preferred_element_type=jnp.float32)


def whiten(place, gram, all_vectors, own, scale):
    vmem = pl.BlockSpec(memory_space=pltpu.VMEM)
    size = gram.shape[0]
    return pl.pallas_call(
        functools.partial(whiten_kernel, scale=scale, panel=4),
        in_specs=[pl.BlockSpec(memory_space=pltpu.SMEM), vmem, vmem],
        out_specs=vmem,
        out_shape=jax.ShapeDtypeStruct((own, all_vectors.shape[1]), jnp.float32),
        scratch_shapes=[pltpu.VMEM((8, size), jnp.float32), pltpu.VMEM((size, size), jnp.float32)],
        compiler_params=pltpu.CompilerParams(vmem_limit_bytes=8 * MIB),
        name="whiten",
    )(place, gram, all_vectors)


def shifted(value, steps):
    count = lax.axis_size(ROWS)
    leading, last = (max(0, -steps), min(count, count - steps))
    return lax.ppermute(value, ROWS, [(source, source + steps) for source in range(leading, last)])


def swapped(value):
    return lax.ppermute(value, "core", [(0, 1), (1, 0)])


def spread(value, axes):
    count = lax.axis_size(axes)
    copies = jnp.broadcast_to(value[None], (count, *value.shape))
    return lax.all_to_all(copies, axes, 0, 0)


def scattered(whole):
    size = whole.shape[0]
    line = lax.axis_size(("z", "core"))
    return lax.all_to_all(whole.reshape(line, size // line, size), ("z", "core"), 0, 0).sum(axis=0)


def gathered(share):
    size = share.shape[1]
    run = spread(share, "y").sum(axis=0)
    return spread(run, ("z", "core")).reshape(size, size)


def body(tile_values, tile_rows, tile_cols, start_vectors):
    own, row_width = start_vectors.shape
    all_count = own * lax.axis_size("x")
    scale = (row_width * lax.axis_size(ROWS)) ** 0.5
    core = lax.axis_index("core").astype(jnp.int32)
    first = core == 0
    place = lax.axis_index("x").astype(jnp.int32).reshape(1)
    core = core.reshape(1)
    bands = operator_band(tile_values, tile_rows, tile_cols, row_width)

    def operator_pass(vectors, beside=()):
        below, above = shifted(vectors, 2), shifted(vectors, -2)
        below, above, *beside = lax.optimization_barrier((below, above, *beside))
        got = swapped(jnp.stack([vectors, jnp.where(first, above, below)]))
        images, kept, crossing, down, up = apply_operator(core, below, above, vectors, got, *bands)
        got = swapped(crossing)
        up = jnp.where(first, up + got[1], up)
        down = jnp.where(first, down, down + got[1])
        return images, kept + got[0] + shifted(up, 2) + shifted(down, -2), beside

    images, pulled, bands = operator_pass(start_vectors, bands)
    all_vectors = spread(pulled, "x").reshape(all_count, row_width)
    share = scattered(gram_share(all_vectors))
    for iteration in range(1, ITERS):
        last = iteration == ITERS - 1
        images, ahead, taken = operator_pass(pulled, [share])
        inverse = cholesky_inverse(gathered(*taken))
        raw = spread(jnp.stack([ahead, images] if last else [ahead]), "x")
        all_vectors, pulled, gram = advance(place, inverse, raw, scale)
        share = scattered(gram)
    images = pulled
    vectors = whiten(place, gathered(share), all_vectors, own, scale)
    return (vectors, images)


def solution(mesh):
    split = Mesh(mesh.devices.reshape(8, 8, 2, 4), ("y", "z", "core", "x"))
    return jax.shard_map(
        body,
        mesh=split,
        in_specs=(P(ROWS, None, None), P(ROWS), P(ROWS), P("x", ROWS)),
        out_specs=(P("x", ROWS), P("x", ROWS)),
        check_vma=False,
    )
```

```python
import functools

import jax
import jax.numpy as jnp
from jax import lax
from jax.experimental import pallas as pl
from jax.experimental.pallas import tpu as pltpu
from jax.sharding import Mesh, PartitionSpec as P


REACH = 2
GROUPS = 2 * REACH + 1
ITERS = 3
ROWS = ("y", "z", "core")
MIB = 1 << 20

precise = lax.Precision.HIGHEST


def halves(value):
    high = value.astype(jnp.bfloat16)
    low = (value - high.astype(jnp.float32)).astype(jnp.bfloat16)
    return high, low


def band_kernel(rows_ref, cols_ref, tiles_hbm, high, low, tiles, total, sems):
    groups, width, _ = high.shape
    slots, size, _ = tiles.shape
    in_group, blocks = slots // groups, width // size
    arrive = []
    for g in range(groups):
        part = pl.ds(g * in_group, in_group)
        arrive.append(pltpu.make_async_copy(tiles_hbm.at[part], tiles.at[part], sems.at[g]))
        arrive[-1].start()
    for g in range(groups):
        arrive[g].wait()
        total[...] = jnp.zeros_like(total)
        for s in range(in_group):
            slot = g * in_group + s
            row, col = rows_ref[slot], cols_ref[slot]

            @pl.when(col >= 0)
            def _():
                at = (
                    pl.ds(pl.multiple_of(row * size, size), size),
                    pl.ds(pl.multiple_of(lax.rem(col, blocks) * size, size), size),
                )
                total[at] += tiles[slot]

        high[g], low[g] = halves(total[...])


def operator_band(tile_values, tile_rows, tile_cols, width):
    smem, vmem = pl.BlockSpec(memory_space=pltpu.SMEM), pl.BlockSpec(memory_space=pltpu.VMEM)
    piece = jax.ShapeDtypeStruct((GROUPS, width, width), jnp.bfloat16)
    return pl.pallas_call(
        band_kernel,
        in_specs=[smem, smem, pl.BlockSpec(memory_space=pl.ANY)],
        out_specs=[vmem, vmem],
        out_shape=[piece, piece],
        scratch_shapes=[
            pltpu.VMEM(tile_values.shape, jnp.float32),
            pltpu.VMEM((width, width), jnp.float32),
            pltpu.SemaphoreType.DMA((GROUPS,)),
        ],
        compiler_params=pltpu.CompilerParams(vmem_limit_bytes=48 * MIB),
        name="operator_band",
    )(tile_rows, tile_cols, tile_values)


def products(high, low, band_high, band_low, dims):
    count = high.shape[0]
    dot = functools.partial(
        lax.dot_general, dimension_numbers=(dims, ((), ())), preferred_element_type=jnp.float32
    )
    both = dot(jnp.concatenate([high, low], axis=0), band_high)
    return both[:count] + both[count:] + dot(high, band_low)


def apply_kernel(core_ref, below, above, own, got, high, low, images, kept, crossing, down, up):
    core = core_ref[0]
    near = [below[...], got[1 - core], own[...], got[core], above[...]]
    total = 0.0
    for g in range(GROUPS):
        total = total + products(*halves(near[g]), high[g], low[g], ((1,), (1,)))
    images[...] = total
    parts = halves(total)
    sent = [products(*parts, high[g], low[g], ((1,), (0,))) for g in range(GROUPS)]
    down[...] = sent[0]
    crossing[1 - core] = sent[1]
    kept[...] = sent[2]
    crossing[core] = sent[3]
    up[...] = sent[4]


def apply_operator(core, below, above, own, got, high, low):
    vmem = pl.BlockSpec(memory_space=pltpu.VMEM)
    one = jax.ShapeDtypeStruct(own.shape, jnp.float32)
    two = jax.ShapeDtypeStruct(got.shape, jnp.float32)
    return pl.pallas_call(
        apply_kernel,
        in_specs=[pl.BlockSpec(memory_space=pltpu.SMEM)] + [vmem] * 6,
        out_specs=[vmem] * 5,
        out_shape=[one, one, two, one, one],
        compiler_params=pltpu.CompilerParams(vmem_limit_bytes=16 * MIB),
        name="apply_operator",
    )(core, below, above, own, got, high, low)


def gram_of(value):
    return lax.dot_general(
        value, value, (((1,), (1,)), ((), ())), precision=precise, preferred_element_type=jnp.float32
    )


def gram_kernel(all_ref, out_ref):
    out_ref[...] = gram_of(all_ref[...])


def gram_share(all_vectors):
    vmem = pl.BlockSpec(memory_space=pltpu.VMEM)
    size = all_vectors.shape[0]
    return pl.pallas_call(
        gram_kernel,
        in_specs=[vmem],
        out_specs=vmem,
        out_shape=jax.ShapeDtypeStruct((size, size), jnp.float32),
        compiler_params=pltpu.CompilerParams(vmem_limit_bytes=8 * MIB),
        name="gram_share",
    )(all_vectors)


def advance_kernel(place_ref, inverse_ref, raw_ref, all_ref, own_ref, gram_ref, *, scale):
    members, parts, own, width = raw_ref.shape
    dot = functools.partial(jnp.dot, precision=precise, preferred_element_type=jnp.float32)
    current = scale * dot(inverse_ref[...], raw_ref[:, 0].reshape(members * own, width))
    all_ref[...] = current
    gram_ref[...] = gram_of(current)
    rows = pl.ds(pl.multiple_of(place_ref[0] * own, own), own)
    if parts == 1:
        own_ref[...] = all_ref[rows, :]
    else:
        last = raw_ref[:, parts - 1].reshape(members * own, width)
        own_ref[...] = scale * dot(inverse_ref[rows, :], last)


def advance(place, inverse, raw, scale):
    vmem = pl.BlockSpec(memory_space=pltpu.VMEM)
    members, _, own, width = raw.shape
    size = members * own
    return pl.pallas_call(
        functools.partial(advance_kernel, scale=scale),
        in_specs=[pl.BlockSpec(memory_space=pltpu.SMEM), vmem, vmem],
        out_specs=[vmem] * 3,
        out_shape=[
            jax.ShapeDtypeStruct((size, width), jnp.float32),
            jax.ShapeDtypeStruct((own, width), jnp.float32),
            jax.ShapeDtypeStruct((size, size), jnp.float32),
        ],
        compiler_params=pltpu.CompilerParams(vmem_limit_bytes=8 * MIB),
        name="advance",
    )(place, inverse, raw)


def invert(gram_ref, inverse_ref, zero_ref, panel):
    size = gram_ref.shape[0]
    tall = 8
    zero_ref[...] = jnp.zeros((tall, size), jnp.float32)
    zero = zero_ref[...]
    row = lax.broadcasted_iota(jnp.int32, (tall, size), 0)
    col = lax.broadcasted_iota(jnp.int32, (tall, size), 1)
    count = size // tall
    left = [gram_ref[tall * b : tall * (b + 1), :] for b in range(count)]
    right = [jnp.where(row + tall * b == col, 1.0, 0.0).astype(jnp.float32) for b in range(count)]

    def lane(value, j):
        return jnp.broadcast_to(value[:, j : j + 1], (tall, size))

    def line(value, i):
        return jnp.broadcast_to(value[i : i + 1, :], (tall, size))

    pivots = jnp.ones((tall, size), jnp.float32)
    for j in range(0, size, panel):
        jb, js = divmod(j, tall)
        low = jb if js + panel < tall else jb + 1
        a = [line(left[jb], js + k) for k in range(panel)]
        w = [line(right[jb], js + k) for k in range(panel)]
        c = [[lane(left[b], j + k) for b in range(low, count)] for k in range(panel)]
        s = {(k, i): lane(a[k] + zero, j + i) for k in range(panel) for i in range(k, panel)}
        factors = []
        for k in range(panel):
            inv = 1.0 / s[k, k]
            pivots = jnp.where(row == js + k, s[k, k], pivots)
            for i in range(k + 1, panel):
                f = s[k, i] * inv
                for i2 in range(i, panel):
                    s[i, i2] = s[i, i2] - f * s[k, i2]
                a[i] = a[i] - f * a[k]
                w[i] = w[i] - f * w[k]
            m = [value * inv for value in c[k]]
            factors.append(m)
            for k2 in range(k + 1, panel):
                c[k2] = [y - x * s[k, k2] for x, y in zip(m, c[k2])]
        for n, b in enumerate(range(low, count)):
            da = dw = 0.0
            for k in range(panel):
                m = factors[k][n]
                if b == jb:
                    m = jnp.where(row > js + panel - 1, m, 0.0)
                da = da + m * a[k]
                dw = dw + m * w[k]
            left[b] = left[b] - da
            right[b] = right[b] - dw
        for k in range(1, panel):
            left[jb] = jnp.where(row == js + k, a[k], left[jb])
            right[jb] = jnp.where(row == js + k, w[k], right[jb])
        if js + panel == tall:
            inverse_ref[tall * jb : tall * (jb + 1), :] = right[jb] * (1.0 / jnp.sqrt(pivots))
            pivots = jnp.ones((tall, size), jnp.float32)


def inverse_kernel(gram_ref, inverse_ref, zero_ref, *, panel):
    invert(gram_ref, inverse_ref, zero_ref, panel)


def cholesky_inverse(gram):
    vmem = pl.BlockSpec(memory_space=pltpu.VMEM)
    return pl.pallas_call(
        functools.partial(inverse_kernel, panel=4),
        in_specs=[vmem],
        out_specs=vmem,
        out_shape=jax.ShapeDtypeStruct(gram.shape, jnp.float32),
        scratch_shapes=[pltpu.VMEM((8, gram.shape[0]), jnp.float32)],
        compiler_params=pltpu.CompilerParams(vmem_limit_bytes=8 * MIB),
        name="cholesky_inverse",
    )(gram)


def whiten_kernel(place_ref, gram_ref, all_ref, out_ref, zero_ref, inverse_ref, *, scale, panel):
    invert(gram_ref, inverse_ref, zero_ref, panel)
    own = out_ref.shape[0]
    rows = inverse_ref[pl.ds(pl.multiple_of(place_ref[0] * own, own), own), :]
    out_ref[...] = scale * jnp.dot(rows, all_ref[...], precision=precise, preferred_element_type=jnp.float32)


def whiten(place, gram, all_vectors, own, scale):
    vmem = pl.BlockSpec(memory_space=pltpu.VMEM)
    size = gram.shape[0]
    return pl.pallas_call(
        functools.partial(whiten_kernel, scale=scale, panel=4),
        in_specs=[pl.BlockSpec(memory_space=pltpu.SMEM), vmem, vmem],
        out_specs=vmem,
        out_shape=jax.ShapeDtypeStruct((own, all_vectors.shape[1]), jnp.float32),
        scratch_shapes=[pltpu.VMEM((8, size), jnp.float32), pltpu.VMEM((size, size), jnp.float32)],
        compiler_params=pltpu.CompilerParams(vmem_limit_bytes=8 * MIB),
        name="whiten",
    )(place, gram, all_vectors)


def shifted(value, steps):
    count = lax.axis_size(ROWS)
    leading, last = (max(0, -steps), min(count, count - steps))
    return lax.ppermute(value, ROWS, [(source, source + steps) for source in range(leading, last)])


def swapped(value):
    return lax.ppermute(value, "core", [(0, 1), (1, 0)])


def spread(value, axes):
    count = lax.axis_size(axes)
    copies = jnp.broadcast_to(value[None], (count, *value.shape))
    return lax.all_to_all(copies, axes, 0, 0)


def scattered(whole):
    size = whole.shape[0]
    line = lax.axis_size(("z", "core"))
    return lax.all_to_all(whole.reshape(line, size // line, size), ("z", "core"), 0, 0).sum(axis=0)


def gathered(share):
    size = share.shape[1]
    run = spread(share, "y").sum(axis=0)
    return spread(run, ("z", "core")).reshape(size, size)


def body(tile_values, tile_rows, tile_cols, start_vectors):
    own, row_width = start_vectors.shape
    all_count = own * lax.axis_size("x")
    scale = (row_width * lax.axis_size(ROWS)) ** 0.5
    core = lax.axis_index("core").astype(jnp.int32)
    first = core == 0
    place = lax.axis_index("x").astype(jnp.int32).reshape(1)
    core = core.reshape(1)
    bands = operator_band(tile_values, tile_rows, tile_cols, row_width)

    def operator_pass(vectors, beside=()):
        below = shifted(vectors, 2)
        above = shifted(vectors, -2)
        below, above, *beside = lax.optimization_barrier((below, above, *beside))
        got = swapped(jnp.stack([vectors, jnp.where(first, above, below)]))
        images, kept, crossing, down, up = apply_operator(core, below, above, vectors, got, *bands)
        got = swapped(crossing)
        up = jnp.where(first, up + got[1], up)
        down = jnp.where(first, down, down + got[1])
        return images, kept + got[0] + shifted(up, 2) + shifted(down, -2), beside

    images, pulled, bands = operator_pass(start_vectors, bands)
    gram = None
    for iteration in range(1, ITERS):
        last = iteration == ITERS - 1
        if gram is None:
            gram = gram_share(spread(pulled, "x").reshape(all_count, row_width))
        share = scattered(gram)
        images, ahead, taken = operator_pass(pulled, [share])
        inverse = cholesky_inverse(gathered(*taken))
        raw = spread(jnp.stack([ahead, images] if last else [ahead]), "x")
        all_vectors, pulled, gram = advance(place, inverse, raw, scale)
    share = scattered(gram)
    images = pulled
    vectors = whiten(place, gathered(share), all_vectors, own, scale)
    return (vectors, images)


def solution(mesh):
    split = Mesh(mesh.devices.reshape(8, 8, 2, 4), ("y", "z", "core", "x"))
    return jax.shard_map(
        body,
        mesh=split,
        in_specs=(P(ROWS, None, None), P(ROWS), P(ROWS), P("x", ROWS)),
        out_specs=(P("x", ROWS), P("x", ROWS)),
        check_vma=False,
    )
```

```python
import functools

import jax
import jax.numpy as jnp
from jax import lax
from jax.experimental import pallas as pl
from jax.experimental.pallas import tpu as pltpu
from jax.sharding import Mesh, PartitionSpec as P

REACH = 2
GROUPS = 2 * REACH + 1
ITERS = 3
ROWS = ("y", "z", "core")
MIB = 1 << 20

precise = lax.Precision.HIGHEST


def halves(value):
    high = value.astype(jnp.bfloat16)
    low = (value - high.astype(jnp.float32)).astype(jnp.bfloat16)
    return high, low


def band_kernel(rows_ref, cols_ref, tiles_hbm, high, low, tiles, total, sems):
    groups, width, _ = high.shape
    slots, size, _ = tiles.shape
    in_group, blocks = slots // groups, width // size
    arrive = []
    for g in range(groups):
        part = pl.ds(g * in_group, in_group)
        arrive.append(pltpu.make_async_copy(tiles_hbm.at[part], tiles.at[part], sems.at[g]))
        arrive[-1].start()
    for g in range(groups):
        arrive[g].wait()
        total[...] = jnp.zeros_like(total)
        for s in range(in_group):
            slot = g * in_group + s
            row, col = rows_ref[slot], cols_ref[slot]

            @pl.when(col >= 0)
            def _():
                at = (
                    pl.ds(pl.multiple_of(row * size, size), size),
                    pl.ds(pl.multiple_of(lax.rem(col, blocks) * size, size), size),
                )
                total[at] += tiles[slot]

        high[g], low[g] = halves(total[...])


def operator_band(tile_values, tile_rows, tile_cols, width):
    smem, vmem = pl.BlockSpec(memory_space=pltpu.SMEM), pl.BlockSpec(memory_space=pltpu.VMEM)
    piece = jax.ShapeDtypeStruct((GROUPS, width, width), jnp.bfloat16)
    return pl.pallas_call(
        band_kernel,
        in_specs=[smem, smem, pl.BlockSpec(memory_space=pl.ANY)],
        out_specs=[vmem, vmem],
        out_shape=[piece, piece],
        scratch_shapes=[
            pltpu.VMEM(tile_values.shape, jnp.float32),
            pltpu.VMEM((width, width), jnp.float32),
            pltpu.SemaphoreType.DMA((GROUPS,)),
        ],
        compiler_params=pltpu.CompilerParams(vmem_limit_bytes=48 * MIB),
        name="operator_band",
    )(tile_rows, tile_cols, tile_values)


def products(high, low, band_high, band_low, dims):
    count = high.shape[0]
    dot = functools.partial(
        lax.dot_general, dimension_numbers=(dims, ((), ())), preferred_element_type=jnp.float32
    )
    both = dot(jnp.concatenate([high, low], axis=0), band_high)
    return both[:count] + both[count:] + dot(high, band_low)


def apply_kernel(core_ref, below, above, own, got, high, low, images, kept, crossing, down, up):
    core = core_ref[0]
    near = [below[...], got[1 - core], own[...], got[core], above[...]]
    total = 0.0
    for g in range(GROUPS):
        total = total + products(*halves(near[g]), high[g], low[g], ((1,), (1,)))
    images[...] = total
    parts = halves(total)
    sent = [products(*parts, high[g], low[g], ((1,), (0,))) for g in range(GROUPS)]
    down[...] = sent[0]
    crossing[1 - core] = sent[1]
    kept[...] = sent[2]
    crossing[core] = sent[3]
    up[...] = sent[4]


def apply_operator(core, below, above, own, got, high, low):
    vmem = pl.BlockSpec(memory_space=pltpu.VMEM)
    one = jax.ShapeDtypeStruct(own.shape, jnp.float32)
    two = jax.ShapeDtypeStruct(got.shape, jnp.float32)
    return pl.pallas_call(
        apply_kernel,
        in_specs=[pl.BlockSpec(memory_space=pltpu.SMEM)] + [vmem] * 6,
        out_specs=[vmem] * 5,
        out_shape=[one, one, two, one, one],
        compiler_params=pltpu.CompilerParams(vmem_limit_bytes=16 * MIB),
        name="apply_operator",
    )(core, below, above, own, got, high, low)


def gram_of(value):
    return lax.dot_general(
        value, value, (((1,), (1,)), ((), ())), precision=precise, preferred_element_type=jnp.float32
    )


def gram_kernel(all_ref, out_ref):
    out_ref[...] = gram_of(all_ref[...])


def gram_share(all_vectors):
    vmem = pl.BlockSpec(memory_space=pltpu.VMEM)
    size = all_vectors.shape[0]
    return pl.pallas_call(
        gram_kernel,
        in_specs=[vmem],
        out_specs=vmem,
        out_shape=jax.ShapeDtypeStruct((size, size), jnp.float32),
        compiler_params=pltpu.CompilerParams(vmem_limit_bytes=8 * MIB),
        name="gram_share",
    )(all_vectors)


def advance_kernel(place_ref, inverse_ref, raw_ref, all_ref, own_ref, gram_ref, *, scale):
    members, parts, own, width = raw_ref.shape
    dot = functools.partial(jnp.dot, precision=precise, preferred_element_type=jnp.float32)
    current = scale * dot(inverse_ref[...], raw_ref[:, 0].reshape(members * own, width))
    all_ref[...] = current
    gram_ref[...] = gram_of(current)
    rows = pl.ds(pl.multiple_of(place_ref[0] * own, own), own)
    if parts == 1:
        own_ref[...] = all_ref[rows, :]
    else:
        last = raw_ref[:, parts - 1].reshape(members * own, width)
        own_ref[...] = scale * dot(inverse_ref[rows, :], last)


def advance(place, inverse, raw, scale):
    vmem = pl.BlockSpec(memory_space=pltpu.VMEM)
    members, _, own, width = raw.shape
    size = members * own
    return pl.pallas_call(
        functools.partial(advance_kernel, scale=scale),
        in_specs=[pl.BlockSpec(memory_space=pltpu.SMEM), vmem, vmem],
        out_specs=[vmem] * 3,
        out_shape=[
            jax.ShapeDtypeStruct((size, width), jnp.float32),
            jax.ShapeDtypeStruct((own, width), jnp.float32),
            jax.ShapeDtypeStruct((size, size), jnp.float32),
        ],
        compiler_params=pltpu.CompilerParams(vmem_limit_bytes=8 * MIB),
        name="advance",
    )(place, inverse, raw)


def invert(gram_ref, inverse_ref, zero_ref, panel):
    size = gram_ref.shape[0]
    tall = 8
    zero_ref[...] = jnp.zeros((tall, size), jnp.float32)
    zero = zero_ref[...]
    row = lax.broadcasted_iota(jnp.int32, (tall, size), 0)
    col = lax.broadcasted_iota(jnp.int32, (tall, size), 1)
    count = size // tall
    left = [gram_ref[tall * b : tall * (b + 1), :] for b in range(count)]
    right = [jnp.where(row + tall * b == col, 1.0, 0.0).astype(jnp.float32) for b in range(count)]

    def lane(value, j):
        return jnp.broadcast_to(value[:, j : j + 1], (tall, size))

    def line(value, i):
        return jnp.broadcast_to(value[i : i + 1, :], (tall, size))

    pivots = jnp.ones((tall, size), jnp.float32)
    for j in range(0, size, panel):
        jb, js = divmod(j, tall)
        low = jb if js + panel < tall else jb + 1
        a = [line(left[jb], js + k) for k in range(panel)]
        w = [line(right[jb], js + k) for k in range(panel)]
        c = [[lane(left[b], j + k) for b in range(low, count)] for k in range(panel)]
        s = {(k, i): lane(a[k] + zero, j + i) for k in range(panel) for i in range(k, panel)}
        factors = []
        for k in range(panel):
            inv = 1.0 / s[k, k]
            pivots = jnp.where(row == js + k, s[k, k], pivots)
            for i in range(k + 1, panel):
                f = s[k, i] * inv
                for i2 in range(i, panel):
                    s[i, i2] = s[i, i2] - f * s[k, i2]
                a[i] = a[i] - f * a[k]
                w[i] = w[i] - f * w[k]
            m = [value * inv for value in c[k]]
            factors.append(m)
            for k2 in range(k + 1, panel):
                c[k2] = [y - x * s[k, k2] for x, y in zip(m, c[k2])]
        for n, b in enumerate(range(low, count)):
            da = dw = 0.0
            for k in range(panel):
                m = factors[k][n]
                if b == jb:
                    m = jnp.where(row > js + panel - 1, m, 0.0)
                da = da + m * a[k]
                dw = dw + m * w[k]
            left[b] = left[b] - da
            right[b] = right[b] - dw
        for k in range(1, panel):
            left[jb] = jnp.where(row == js + k, a[k], left[jb])
            right[jb] = jnp.where(row == js + k, w[k], right[jb])
        if js + panel == tall:
            inverse_ref[tall * jb : tall * (jb + 1), :] = right[jb] * (1.0 / jnp.sqrt(pivots))
            pivots = jnp.ones((tall, size), jnp.float32)


def inverse_kernel(gram_ref, inverse_ref, zero_ref, *, panel):
    invert(gram_ref, inverse_ref, zero_ref, panel)


def cholesky_inverse(gram):
    vmem = pl.BlockSpec(memory_space=pltpu.VMEM)
    return pl.pallas_call(
        functools.partial(inverse_kernel, panel=4),
        in_specs=[vmem],
        out_specs=vmem,
        out_shape=jax.ShapeDtypeStruct(gram.shape, jnp.float32),
        scratch_shapes=[pltpu.VMEM((8, gram.shape[0]), jnp.float32)],
        compiler_params=pltpu.CompilerParams(vmem_limit_bytes=8 * MIB),
        name="cholesky_inverse",
    )(gram)


def whiten_kernel(place_ref, gram_ref, all_ref, out_ref, zero_ref, inverse_ref, *, scale, panel):
    invert(gram_ref, inverse_ref, zero_ref, panel)
    own = out_ref.shape[0]
    rows = inverse_ref[pl.ds(pl.multiple_of(place_ref[0] * own, own), own), :]
    out_ref[...] = scale * jnp.dot(rows, all_ref[...], precision=precise, preferred_element_type=jnp.float32)


def whiten(place, gram, all_vectors, own, scale):
    vmem = pl.BlockSpec(memory_space=pltpu.VMEM)
    size = gram.shape[0]
    return pl.pallas_call(
        functools.partial(whiten_kernel, scale=scale, panel=4),
        in_specs=[pl.BlockSpec(memory_space=pltpu.SMEM), vmem, vmem],
        out_specs=vmem,
        out_shape=jax.ShapeDtypeStruct((own, all_vectors.shape[1]), jnp.float32),
        scratch_shapes=[pltpu.VMEM((8, size), jnp.float32), pltpu.VMEM((size, size), jnp.float32)],
        compiler_params=pltpu.CompilerParams(vmem_limit_bytes=8 * MIB),
        name="whiten",
    )(place, gram, all_vectors)


def shifted(value, steps):
    count = lax.axis_size(ROWS)
    leading, last = (max(0, -steps), min(count, count - steps))
    return lax.ppermute(value, ROWS, [(source, source + steps) for source in range(leading, last)])


def swapped(value):
    return lax.ppermute(value, "core", [(0, 1), (1, 0)])


def spread(value, axes):
    count = lax.axis_size(axes)
    copies = jnp.broadcast_to(value[None], (count, *value.shape))
    return lax.all_to_all(copies, axes, 0, 0)


def scattered(whole):
    size = whole.shape[0]
    line = lax.axis_size(("z", "core"))
    share = lax.all_to_all(whole.reshape(line, size // line, size), ("z", "core"), 0, 0).sum(axis=0)
    return spread(share, "y").sum(axis=0)


def gathered(share):
    size = share.shape[1]
    return spread(share, ("z", "core")).reshape(size, size)


def body(tile_values, tile_rows, tile_cols, start_vectors):
    own, row_width = start_vectors.shape
    all_count = own * lax.axis_size("x")
    scale = (row_width * lax.axis_size(ROWS)) ** 0.5
    core = lax.axis_index("core").astype(jnp.int32)
    first = core == 0
    place = lax.axis_index("x").astype(jnp.int32).reshape(1)
    core = core.reshape(1)
    bands = operator_band(tile_values, tile_rows, tile_cols, row_width)

    def operator_pass(vectors, beside=()):
        below, above = shifted(vectors, 2), shifted(vectors, -2)
        below, above, *beside = lax.optimization_barrier((below, above, *beside))
        got = swapped(jnp.stack([vectors, jnp.where(first, above, below)]))
        images, kept, crossing, down, up = apply_operator(core, below, above, vectors, got, *bands)
        got = swapped(crossing)
        up = jnp.where(first, up + got[1], up)
        down = jnp.where(first, down, down + got[1])
        return images, kept + got[0] + shifted(up, 2) + shifted(down, -2), beside

    images, pulled, bands = operator_pass(start_vectors, bands)
    all_vectors = spread(pulled, "x").reshape(all_count, row_width)
    share = scattered(gram_share(all_vectors))
    for iteration in range(1, ITERS):
        last = iteration == ITERS - 1
        images, ahead, taken = operator_pass(pulled, [share])
        inverse = cholesky_inverse(gathered(*taken))
        raw = spread(jnp.stack([ahead, images] if last else [ahead]), "x")
        all_vectors, pulled, gram = advance(place, inverse, raw, scale)
        share = scattered(gram)
    images = pulled
    vectors = whiten(place, gathered(share), all_vectors, own, scale)
    return (vectors, images)


def solution(mesh):
    split = Mesh(mesh.devices.reshape(8, 8, 2, 4), ("y", "z", "core", "x"))
    return jax.shard_map(
        body,
        mesh=split,
        in_specs=(P(ROWS, None, None), P(ROWS), P(ROWS), P("x", ROWS)),
        out_specs=(P("x", ROWS), P("x", ROWS)),
        check_vma=False,
    )
```
